128 devices in a mesh: layer: 16 (over x, y_hi, core), row: 8 (over y_lo, z).
Axes of the slice: x: 4, y: 4 (y_hi: 2, y_lo: 2; y = y_hi * 2 + y_lo), z: 4, core: 2. Of those that a mesh axis runs over, the one named last changes fastest.
Arguments:
- operator: bfloat16 [2, 16, 4096, 4096], P(None, 'layer', 'row'), may hold values from -0.0625 to 0.0625
- sources: bfloat16 [2, 16, 4096, 512], P(None, 'layer', 'row'), may hold values from -3 to 3
- boundary: bfloat16 [2, 4096, 512], P(None, 'row'), may hold values from -6 to 6
Outputs:
- traces: float32 [2, 16, 4096, 512], P(None, 'layer', 'row')
The draws below stay inside these ranges and needn't reach their ends.
All inputs are finite; a program needn't handle non-finite values.
Results may differ from the reference program's by a relative error of at most 0.015.
Values may be sent and summed in bfloat16 or wider, within the bound.
No kernel may reach another device: no remote copies, remote signals or barrier semaphores. Data moves between devices by JAX's collectives and lax.ppermute only.
A program may use at most 64 MiB of HBM per device.

```python
import jax
import jax.numpy as jnp

M = 4096
SRC = 512
LAYERS = 16


def level_of(own_key, shape, pieces, low, high):
    level, own = 1.0, jax.random.fold_in(own_key, 6)
    for dim, blocks in pieces:
        draws = jnp.exp(jax.random.uniform(jax.random.fold_in(own, dim), (blocks,), jnp.float32, low / len(pieces), high / len(pieces)))
        level = level * jnp.repeat(draws, shape[dim] // blocks).reshape([-1 if axis == dim else 1 for axis in range(len(shape))])
    return level


def centred(key, extent, spread, limit, shards=(), held_as=jnp.bfloat16):
    array = spread * jax.random.normal(key, extent, jnp.float32)
    if shards:
        array = array * level_of(key, extent, shards, -0.22, 0.18)
    return jnp.clip(array, -limit, limit).astype(held_as)


def setup_inputs(seed: int = 0) -> dict:
    seeds = jax.random.split(jax.random.key(seed), 4)
    operator = centred(seeds[0], (2, LAYERS, M, M), (2 * M) ** -0.5, 0.0625, ((1, 16), (2, 8)))
    sources = centred(seeds[1], (2, LAYERS, M, SRC), 0.5, 3.0, ((1, 16), (2, 8)))
    boundary = centred(seeds[2], (2, M, SRC), 1.0, 6.0, ((1, 8),))
    return dict(operator=operator, sources=sources, boundary=boundary)


def reference(operator, sources, boundary):
    incoming = boundary
    outputs = []
    for level in range(LAYERS):
        real = operator[0, level]
        imag = operator[1, level]
        part_re = jnp.dot(real, incoming[0], preferred_element_type=jnp.float32) - jnp.dot(imag, incoming[1], preferred_element_type=jnp.float32)
        part_im = jnp.dot(real, incoming[1], preferred_element_type=jnp.float32) + jnp.dot(imag, incoming[0], preferred_element_type=jnp.float32)
        result = jnp.stack([part_re, part_im], axis=0) + sources[:, level].astype(jnp.float32)
        outputs.append(result)
        incoming = result.astype(jnp.bfloat16)
    return jnp.stack(outputs, axis=1)
```

```python
import functools

import jax
import jax.numpy as jnp
from jax import lax
from jax.experimental import pallas as pl
from jax.experimental.pallas import tpu as pltpu
from jax.sharding import PartitionSpec as P

WIDTH = 64
TILE = 256
ONWARD = True
VMEM_LIMIT = 24 * 2**20


def transpose_kernel(turn, order_ref, core_ref, own_ref, other_ref, turned_ref):
    parts, rows, total = own_ref.shape
    across = lax.broadcasted_iota(jnp.int32, (TILE, TILE), 0)
    along = lax.broadcasted_iota(jnp.int32, (TILE, TILE), 1)
    unit = (across == along).astype(jnp.bfloat16)

    def transpose(operator_ref):
        for part in range(parts):
            for start in range(0, total, TILE):
                turned = lax.dot_general(
                    unit,
                    operator_ref[part, :, start : start + TILE],
                    (((1,), (1,)), ((), ())),
                    preferred_element_type=jnp.float32,
                )
                turned_ref[part, start : start + TILE, :] = turned.astype(jnp.bfloat16)

    @pl.when(core_ref[0] == turn)
    def _():
        transpose(own_ref)

    @pl.when(core_ref[0] != turn)
    def _():
        transpose(other_ref)


def transposed(turn, order, core, own, other):
    parts, rows, total = own.shape
    block = pl.BlockSpec((parts, rows, rows), lambda slot, order, core: (0, 0, order[slot]))
    return pl.pallas_call(
        functools.partial(transpose_kernel, turn),
        out_shape=jax.ShapeDtypeStruct((parts, total, rows), own.dtype),
        grid_spec=pltpu.PrefetchScalarGridSpec(
            num_scalar_prefetch=2,
            grid=(total // rows,),
            in_specs=[block, block],
            out_specs=pl.BlockSpec((parts, rows, rows), lambda slot, order, core: (0, slot, 0)),
        ),
        compiler_params=pltpu.CompilerParams(vmem_limit_bytes=VMEM_LIMIT),
        cost_estimate=pl.CostEstimate(flops=1 << 31, bytes_accessed=16 << 20, transcendentals=0),
    )(order, core, own, other)


def layer_kernel(*refs):
    *block_refs, operator_ref, source_ref, full_ref, short_ref, values_ref = refs
    lanes, rows = full_ref.shape
    width = lanes // 2
    for block, ref in enumerate(block_refs):
        values_ref[:, block * rows : (block + 1) * rows] = ref[...]

    def multiply(step, carry):
        columns = pl.ds(pl.multiple_of(step * TILE, TILE), TILE)
        values = values_ref[...]
        by_real = jnp.dot(values, operator_ref[0, :, columns], preferred_element_type=jnp.float32)
        by_imag = jnp.dot(values, operator_ref[1, :, columns], preferred_element_type=jnp.float32)
        total = jnp.concatenate(
            [by_real[:width] - by_imag[width:], by_real[width:] + by_imag[:width]], axis=0
        ) + source_ref[:, columns].astype(jnp.float32)
        full_ref[:, columns] = total
        short_ref[:, columns] = total.astype(jnp.bfloat16)
        return carry

    lax.fori_loop(0, rows // TILE, multiply, 0)


def layer(blocks, operator, source):
    lanes, rows = source.shape
    vmem = pl.BlockSpec(memory_space=pltpu.VMEM)
    return pl.pallas_call(
        layer_kernel,
        out_shape=(
            jax.ShapeDtypeStruct((lanes, rows), jnp.float32),
            jax.ShapeDtypeStruct((lanes, rows), jnp.bfloat16),
        ),
        in_specs=[vmem] * (len(blocks) + 2),
        out_specs=(vmem, vmem),
        scratch_shapes=[pltpu.VMEM((lanes, len(blocks) * rows), jnp.bfloat16)],
        compiler_params=pltpu.CompilerParams(vmem_limit_bytes=VMEM_LIMIT),
        cost_estimate=pl.CostEstimate(
            flops=4 * len(blocks) * rows * rows * lanes, bytes_accessed=1 << 20, transcendentals=0
        ),
    )(*blocks, operator, source)


def batched(array, width):
    parts, rows, columns = array.shape
    split = array.reshape(parts, rows, columns // width, width)
    return jnp.transpose(split, (2, 0, 3, 1)).reshape(columns // width, parts * width, rows)


def unbatched(array, parts):
    count, lanes, rows = array.shape
    split = array.reshape(count, parts, lanes // parts, rows)
    return jnp.transpose(split, (1, 3, 0, 2)).reshape(parts, rows, count * lanes // parts)


def on_device(operator, sources, boundary):
    rows = operator.shape[2]
    total = sources.shape[3]
    layers = lax.axis_size("layer")
    devices = lax.axis_size("row")
    stages = layers // 2
    level = lax.axis_index("layer")
    core = level % 2
    stage = level // 2
    half = total // 2
    width = WIDTH
    count = half // width
    beats = count + stages - 1
    swap = [(i, i ^ 1) for i in range(layers)]

    def exchanged(value, distance):
        return lax.ppermute(value, "row", [(r, r ^ distance) for r in range(devices)])

    def onward(value, distance):
        if ONWARD:
            pairs = [
                (i * devices + r, (i + 2) % layers * devices + (r ^ distance))
                for i in range(layers)
                for r in range(devices)
            ]
            return lax.ppermute(value, ("layer", "row"), pairs)
        return lax.ppermute(value, "layer", [(i, (i + 2) % layers) for i in range(layers)])

    def spread(near, far):
        slots = {0: near, 4: far}
        for distance in (1, 3, 2):
            slots[distance] = exchanged(near, distance)
        for distance in (1, 3, 2):
            slots[4 ^ distance] = exchanged(far, distance)
        return [slots[slot] for slot in range(devices)]

    own = operator[:, 0]
    other = lax.ppermute(own, "layer", swap)
    row = lax.axis_index("row").astype(jnp.int32)
    order = row ^ jnp.arange(devices, dtype=jnp.int32)
    which = core.astype(jnp.int32)[None]
    operators = [transposed(turn, order, which, own, other) for turn in range(2)]

    entering = batched(lax.dynamic_slice_in_dim(boundary, core * half, half, 2), width)
    entering_far = exchanged(entering, 4)
    own_sources = sources[:, 0]
    mine = lax.dynamic_slice_in_dim(own_sources, core * half, half, 2)
    theirs = lax.ppermute(
        lax.dynamic_slice_in_dim(own_sources, (1 - core) * half, half, 2), "layer", swap
    )
    first_sources = batched(jnp.where(core == 0, mine, theirs), width)
    second_sources = batched(jnp.where(core == 0, theirs, mine), width)

    near = far = None
    firsts = jnp.zeros((count, 2 * width, rows), jnp.float32)
    seconds = jnp.zeros((count, 2 * width, rows), jnp.float32)
    for step in range(beats):
        batch = step - stage
        place = jnp.clip(batch, 0, count - 1)
        working = jnp.logical_and(batch >= 0, batch < count)
        if step == 0:
            near, far = entering[0], entering_far[0]
        elif step < count:
            near = jnp.where(stage == 0, entering[step], near)
            far = jnp.where(stage == 0, entering_far[step], far)
        first, middle = layer(spread(near, far), operators[0], first_sources[place])
        gathered = spread(middle, exchanged(middle, 4))
        second, leaving = layer(gathered, operators[1], second_sources[place])
        if step < beats - 1:
            near = onward(leaving, 0)
            far = onward(leaving, 4)
        first = jnp.where(working, first, firsts[place])
        second = jnp.where(working, second, seconds[place])
        firsts = lax.dynamic_update_index_in_dim(firsts, first, place, 0)
        seconds = lax.dynamic_update_index_in_dim(seconds, second, place, 0)

    kept = jnp.where(core == 0, firsts, seconds)
    given = lax.ppermute(jnp.where(core == 0, seconds, firsts), "layer", swap)
    kept = unbatched(kept, 2)
    given = unbatched(given, 2)
    low = jnp.where(core == 0, kept, given)
    high = jnp.where(core == 0, given, kept)
    return jnp.concatenate([low, high], axis=2)[:, None]


def solution(mesh):
    placed = (P(None, "layer", "row", None), P(None, "layer", "row", None), P(None, "row", None))
    return jax.shard_map(
        on_device,
        mesh=mesh,
        in_specs=placed,
        out_specs=P(None, "layer", "row", None),
        check_vma=False,
    )
```

```python
import functools

import jax
import jax.numpy as jnp
from jax import lax
from jax.experimental import pallas as pl
from jax.experimental.pallas import tpu as pltpu
from jax.sharding import PartitionSpec as P

WIDTH = 64
TILE = 256
ONWARD = True
VMEM_LIMIT = 24 * 2**20


def transpose_kernel(order_ref, operator_ref, turned_ref):
    parts, rows, total = operator_ref.shape
    across = lax.broadcasted_iota(jnp.int32, (TILE, TILE), 0)
    along = lax.broadcasted_iota(jnp.int32, (TILE, TILE), 1)
    unit = (across == along).astype(jnp.bfloat16)
    for part in range(parts):
        for start in range(0, total, TILE):
            turned = lax.dot_general(
                unit,
                operator_ref[part, :, start : start + TILE],
                (((1,), (1,)), ((), ())),
                preferred_element_type=jnp.float32,
            )
            turned_ref[part, start : start + TILE, :] = turned.astype(jnp.bfloat16)


def transposed(order, operator):
    parts, rows, total = operator.shape
    return pl.pallas_call(
        transpose_kernel,
        out_shape=jax.ShapeDtypeStruct((parts, total, rows), operator.dtype),
        grid_spec=pltpu.PrefetchScalarGridSpec(
            num_scalar_prefetch=1,
            grid=(total // rows,),
            in_specs=[pl.BlockSpec((parts, rows, rows), lambda slot, order: (0, 0, order[slot]))],
            out_specs=pl.BlockSpec((parts, rows, rows), lambda slot, order: (0, slot, 0)),
        ),
        compiler_params=pltpu.CompilerParams(vmem_limit_bytes=60 * 2**20),
        cost_estimate=pl.CostEstimate(flops=1 << 31, bytes_accessed=16 << 20, transcendentals=0),
    )(order, operator)


def layer_kernel(*refs):
    *block_refs, operator_ref, source_ref, full_ref, short_ref, values_ref = refs
    lanes, rows = full_ref.shape
    width = lanes // 2
    for block, ref in enumerate(block_refs):
        values_ref[:, block * rows : (block + 1) * rows] = ref[...]

    def multiply(step, carry):
        columns = pl.ds(pl.multiple_of(step * TILE, TILE), TILE)
        values = values_ref[...]
        by_real = jnp.dot(values, operator_ref[0, :, columns], preferred_element_type=jnp.float32)
        by_imag = jnp.dot(values, operator_ref[1, :, columns], preferred_element_type=jnp.float32)
        total = jnp.concatenate(
            [by_real[:width] - by_imag[width:], by_real[width:] + by_imag[:width]], axis=0
        ) + source_ref[:, columns].astype(jnp.float32)
        full_ref[:, columns] = total
        short_ref[:, columns] = total.astype(jnp.bfloat16)
        return carry

    lax.fori_loop(0, rows // TILE, multiply, 0)


def layer(blocks, operator, source):
    lanes, rows = source.shape
    vmem = pl.BlockSpec(memory_space=pltpu.VMEM)
    return pl.pallas_call(
        layer_kernel,
        out_shape=(
            jax.ShapeDtypeStruct((lanes, rows), jnp.float32),
            jax.ShapeDtypeStruct((lanes, rows), jnp.bfloat16),
        ),
        in_specs=[vmem] * (len(blocks) + 2),
        out_specs=(vmem, vmem),
        scratch_shapes=[pltpu.VMEM((lanes, len(blocks) * rows), jnp.bfloat16)],
        compiler_params=pltpu.CompilerParams(vmem_limit_bytes=VMEM_LIMIT),
        cost_estimate=pl.CostEstimate(
            flops=4 * len(blocks) * rows * rows * lanes, bytes_accessed=1 << 20, transcendentals=0
        ),
    )(*blocks, operator, source)


def batched(array, width):
    parts, rows, columns = array.shape
    split = array.reshape(parts, rows, columns // width, width)
    return jnp.transpose(split, (2, 0, 3, 1)).reshape(columns // width, parts * width, rows)


def unbatched(array, parts):
    count, lanes, rows = array.shape
    split = array.reshape(count, parts, lanes // parts, rows)
    return jnp.transpose(split, (1, 3, 0, 2)).reshape(parts, rows, count * lanes // parts)


def on_device(operator, sources, boundary):
    rows = operator.shape[2]
    total = sources.shape[3]
    layers = lax.axis_size("layer")
    devices = lax.axis_size("row")
    stages = layers // 2
    level = lax.axis_index("layer")
    core = level % 2
    stage = level // 2
    half = total // 2
    width = WIDTH
    count = half // width
    beats = count + stages - 1
    swap = [(i, i ^ 1) for i in range(layers)]

    def exchanged(value, distance):
        return lax.ppermute(value, "row", [(r, r ^ distance) for r in range(devices)])

    def onward(value, distance):
        if ONWARD:
            pairs = [
                (i * devices + r, (i + 2) % layers * devices + (r ^ distance))
                for i in range(layers)
                for r in range(devices)
            ]
            return lax.ppermute(value, ("layer", "row"), pairs)
        return lax.ppermute(value, "layer", [(i, (i + 2) % layers) for i in range(layers)])

    def spread(near, far):
        slots = {0: near}
        slots[1] = exchanged(near, 1)
        slots[3] = exchanged(near, 3)
        slots[2] = exchanged(near, 2)
        slots[4] = far
        slots[5] = exchanged(far, 1)
        slots[7] = exchanged(far, 3)
        slots[6] = exchanged(slots[2], 4)
        return [slots[slot] for slot in range(devices)]

    def turned_round(slots):
        return [slots[slot ^ 4] for slot in range(devices)]

    row = lax.axis_index("row").astype(jnp.int32)
    order = row ^ jnp.arange(devices, dtype=jnp.int32)
    own = transposed(order, operator[:, 0])
    other = lax.ppermute(own, "layer", swap)
    operators = [jnp.where(core == 0, own, other), jnp.where(core == 0, other, own)]

    entering = batched(lax.dynamic_slice_in_dim(boundary, core * half, half, 2), width)
    entering_far = exchanged(entering, 4)
    own_sources = sources[:, 0]
    mine = lax.dynamic_slice_in_dim(own_sources, core * half, half, 2)
    theirs = lax.ppermute(
        lax.dynamic_slice_in_dim(own_sources, (1 - core) * half, half, 2), "layer", swap
    )
    first_sources = batched(jnp.where(core == 0, mine, theirs), width)
    second_sources = batched(jnp.where(core == 0, theirs, mine), width)

    near = far = None
    firsts = jnp.zeros((count, 2 * width, rows), jnp.float32)
    seconds = jnp.zeros((count, 2 * width, rows), jnp.float32)
    for step in range(beats):
        batch = step - stage
        place = jnp.clip(batch, 0, count - 1)
        working = jnp.logical_and(batch >= 0, batch < count)
        if step == 0:
            near, far = entering[0], entering_far[0]
        elif step < count:
            near = jnp.where(stage == 0, entering[step], near)
            far = jnp.where(stage == 0, entering_far[step], far)
        first, middle = layer(turned_round(spread(far, near)), operators[0], first_sources[place])
        gathered = spread(middle, exchanged(middle, 4))
        second, leaving = layer(gathered, operators[1], second_sources[place])
        if step < beats - 1:
            near = onward(leaving, 0)
            far = onward(leaving, 4)
        first = jnp.where(working, first, firsts[place])
        second = jnp.where(working, second, seconds[place])
        firsts = lax.dynamic_update_index_in_dim(firsts, first, place, 0)
        seconds = lax.dynamic_update_index_in_dim(seconds, second, place, 0)

    kept = jnp.where(core == 0, firsts, seconds)
    given = lax.ppermute(jnp.where(core == 0, seconds, firsts), "layer", swap)
    kept = unbatched(kept, 2)
    given = unbatched(given, 2)
    low = jnp.where(core == 0, kept, given)
    high = jnp.where(core == 0, given, kept)
    return jnp.concatenate([low, high], axis=2)[:, None]


def solution(mesh):
    placed = (P(None, "layer", "row", None), P(None, "layer", "row", None), P(None, "row", None))
    return jax.shard_map(
        on_device,
        mesh=mesh,
        in_specs=placed,
        out_specs=P(None, "layer", "row", None),
        check_vma=False,
    )
```

```python
import functools

import jax
import jax.numpy as jnp
from jax import lax
from jax.experimental import pallas as pl
from jax.experimental.pallas import tpu as pltpu
from jax.sharding import PartitionSpec as P

WIDTH = 64
TILE = 256
ONWARD = True
VMEM_LIMIT = 24 * 2**20


def transpose_kernel(order_ref, operator_ref, turned_ref):
    parts, rows, total = operator_ref.shape
    across = lax.broadcasted_iota(jnp.int32, (TILE, TILE), 0)
    along = lax.broadcasted_iota(jnp.int32, (TILE, TILE), 1)
    unit = (across == along).astype(jnp.bfloat16)
    for part in range(parts):
        for start in range(0, total, TILE):
            turned = lax.dot_general(
                unit,
                operator_ref[part, :, start : start + TILE],
                (((1,), (1,)), ((), ())),
                preferred_element_type=jnp.float32,
            )
            turned_ref[part, start : start + TILE, :] = turned.astype(jnp.bfloat16)


def transposed(order, operator):
    parts, rows, total = operator.shape
    return pl.pallas_call(
        transpose_kernel,
        out_shape=jax.ShapeDtypeStruct((parts, total, rows), operator.dtype),
        grid_spec=pltpu.PrefetchScalarGridSpec(
            num_scalar_prefetch=1,
            grid=(total // rows,),
            in_specs=[pl.BlockSpec((parts, rows, rows), lambda slot, order: (0, 0, order[slot]))],
            out_specs=pl.BlockSpec((parts, rows, rows), lambda slot, order: (0, slot, 0)),
        ),
        compiler_params=pltpu.CompilerParams(vmem_limit_bytes=60 * 2**20),
        cost_estimate=pl.CostEstimate(flops=1 << 31, bytes_accessed=16 << 20, transcendentals=0),
    )(order, operator)


def layer_kernel(*refs):
    *block_refs, operator_ref, source_ref, full_ref, short_ref, values_ref = refs
    lanes, rows = full_ref.shape
    width = lanes // 2
    for block, ref in enumerate(block_refs):
        values_ref[:, block * rows : (block + 1) * rows] = ref[...]

    def multiply(step, carry):
        columns = pl.ds(pl.multiple_of(step * TILE, TILE), TILE)
        values = values_ref[...]
        by_real = jnp.dot(values, operator_ref[0, :, columns], preferred_element_type=jnp.float32)
        by_imag = jnp.dot(values, operator_ref[1, :, columns], preferred_element_type=jnp.float32)
        total = jnp.concatenate(
            [by_real[:width] - by_imag[width:], by_real[width:] + by_imag[:width]], axis=0
        ) + source_ref[:, columns].astype(jnp.float32)
        full_ref[:, columns] = total
        short_ref[:, columns] = total.astype(jnp.bfloat16)
        return carry

    lax.fori_loop(0, rows // TILE, multiply, 0)


def layer(blocks, operator, source):
    lanes, rows = source.shape
    vmem = pl.BlockSpec(memory_space=pltpu.VMEM)
    return pl.pallas_call(
        layer_kernel,
        out_shape=(
            jax.ShapeDtypeStruct((lanes, rows), jnp.float32),
            jax.ShapeDtypeStruct((lanes, rows), jnp.bfloat16),
        ),
        in_specs=[vmem] * (len(blocks) + 2),
        out_specs=(vmem, vmem),
        scratch_shapes=[pltpu.VMEM((lanes, len(blocks) * rows), jnp.bfloat16)],
        compiler_params=pltpu.CompilerParams(vmem_limit_bytes=VMEM_LIMIT),
        cost_estimate=pl.CostEstimate(
            flops=4 * len(blocks) * rows * rows * lanes, bytes_accessed=1 << 20, transcendentals=0
        ),
    )(*blocks, operator, source)


def batched(array, width):
    parts, rows, columns = array.shape
    split = array.reshape(parts, rows, columns // width, width)
    return jnp.transpose(split, (2, 0, 3, 1)).reshape(columns // width, parts * width, rows)


def unbatched(array, parts):
    count, lanes, rows = array.shape
    split = array.reshape(count, parts, lanes // parts, rows)
    return jnp.transpose(split, (1, 3, 0, 2)).reshape(parts, rows, count * lanes // parts)


def on_device(operator, sources, boundary):
    rows = operator.shape[2]
    total = sources.shape[3]
    layers = lax.axis_size("layer")
    devices = lax.axis_size("row")
    stages = layers // 2
    level = lax.axis_index("layer")
    core = level % 2
    stage = level // 2
    half = total // 2
    width = WIDTH
    count = half // width
    beats = count + stages - 1
    swap = [(i, i ^ 1) for i in range(layers)]

    def exchanged(value, distance):
        return lax.ppermute(value, "row", [(r, r ^ distance) for r in range(devices)])

    def onward(value, distance):
        if ONWARD:
            pairs = [
                (i * devices + r, (i + 2) % layers * devices + (r ^ distance))
                for i in range(layers)
                for r in range(devices)
            ]
            return lax.ppermute(value, ("layer", "row"), pairs)
        return lax.ppermute(value, "layer", [(i, (i + 2) % layers) for i in range(layers)])

    def spread(near, far):
        slots = {0: near}
        slots[1] = exchanged(near, 1)
        slots[3] = exchanged(near, 3)
        slots[2] = exchanged(near, 2)
        slots[4] = far
        slots[5] = exchanged(far, 1)
        slots[7] = exchanged(far, 3)
        slots[6] = exchanged(slots[2], 4)
        return [slots[slot] for slot in range(devices)]

    def turned_round(slots):
        return [slots[slot ^ 4] for slot in range(devices)]

    row = lax.axis_index("row").astype(jnp.int32)
    order = row ^ jnp.arange(devices, dtype=jnp.int32)
    own = transposed(order, operator[:, 0])
    other = lax.ppermute(own, "layer", swap)
    first_operator = jnp.where(core == 0, own, other)

    entering = batched(lax.dynamic_slice_in_dim(boundary, core * half, half, 2), width)
    opening_far = exchanged(entering[0], 4)
    entering_far = exchanged(entering[1:], 4)
    own_sources = sources[:, 0]
    mine = lax.dynamic_slice_in_dim(own_sources, core * half, half, 2)
    theirs = lax.ppermute(
        lax.dynamic_slice_in_dim(own_sources, (1 - core) * half, half, 2), "layer", swap
    )
    first_sources = batched(jnp.where(core == 0, mine, theirs), width)
    second_sources = batched(jnp.where(core == 0, theirs, mine), width)

    near = far = None
    firsts = jnp.zeros((count, 2 * width, rows), jnp.float32)
    seconds = jnp.zeros((count, 2 * width, rows), jnp.float32)
    for step in range(beats):
        batch = step - stage
        place = jnp.clip(batch, 0, count - 1)
        working = jnp.logical_and(batch >= 0, batch < count)
        if step == 0:
            slots = spread(entering[0], opening_far)
        else:
            if step < count:
                near = jnp.where(stage == 0, entering[step], near)
                far = jnp.where(stage == 0, entering_far[step - 1], far)
            slots = turned_round(spread(far, near))
        first, middle = layer(slots, first_operator, first_sources[place])
        if step == 0:
            later_own, later_other, _ = lax.optimization_barrier((own, other, middle))
            second_operator = jnp.where(core == 0, later_other, later_own)
        gathered = spread(middle, exchanged(middle, 4))
        second, leaving = layer(gathered, second_operator, second_sources[place])
        if step < beats - 1:
            near = onward(leaving, 0)
            far = onward(leaving, 4)
        first = jnp.where(working, first, firsts[place])
        second = jnp.where(working, second, seconds[place])
        firsts = lax.dynamic_update_index_in_dim(firsts, first, place, 0)
        seconds = lax.dynamic_update_index_in_dim(seconds, second, place, 0)

    kept = jnp.where(core == 0, firsts, seconds)
    given = lax.ppermute(jnp.where(core == 0, seconds, firsts), "layer", swap)
    kept = unbatched(kept, 2)
    given = unbatched(given, 2)
    low = jnp.where(core == 0, kept, given)
    high = jnp.where(core == 0, given, kept)
    return jnp.concatenate([low, high], axis=2)[:, None]


def solution(mesh):
    placed = (P(None, "layer", "row", None), P(None, "layer", "row", None), P(None, "row", None))
    return jax.shard_map(
        on_device,
        mesh=mesh,
        in_specs=placed,
        out_specs=P(None, "layer", "row", None),
        check_vma=False,
    )
```

```python
import functools

import jax
import jax.numpy as jnp
from jax import lax
from jax.experimental import pallas as pl
from jax.experimental.pallas import tpu as pltpu
from jax.sharding import PartitionSpec as P

WIDTH = 64
TILE = 256
ONWARD = True
VMEM_LIMIT = 24 * 2**20


def transpose_kernel(order_ref, operator_ref, turned_ref):
    parts, rows, total = operator_ref.shape
    across = lax.broadcasted_iota(jnp.int32, (TILE, TILE), 0)
    along = lax.broadcasted_iota(jnp.int32, (TILE, TILE), 1)
    unit = (across == along).astype(jnp.bfloat16)
    for part in range(parts):
        for start in range(0, total, TILE):
            turned = lax.dot_general(
                unit,
                operator_ref[part, :, start : start + TILE],
                (((1,), (1,)), ((), ())),
                preferred_element_type=jnp.float32,
            )
            turned_ref[part, start : start + TILE, :] = turned.astype(jnp.bfloat16)


def transposed(order, operator):
    parts, rows, total = operator.shape
    return pl.pallas_call(
        transpose_kernel,
        out_shape=jax.ShapeDtypeStruct((parts, total, rows), operator.dtype),
        grid_spec=pltpu.PrefetchScalarGridSpec(
            num_scalar_prefetch=1,
            grid=(total // rows,),
            in_specs=[pl.BlockSpec((parts, rows, rows), lambda slot, order: (0, 0, order[slot]))],
            out_specs=pl.BlockSpec((parts, rows, rows), lambda slot, order: (0, slot, 0)),
        ),
        compiler_params=pltpu.CompilerParams(vmem_limit_bytes=VMEM_LIMIT),
        cost_estimate=pl.CostEstimate(flops=1 << 31, bytes_accessed=16 << 20, transcendentals=0),
    )(order, operator)


def layer_kernel(*refs):
    *block_refs, operator_ref, source_ref, full_ref, short_ref, values_ref = refs
    lanes, rows = full_ref.shape
    width = lanes // 2
    for block, ref in enumerate(block_refs):
        values_ref[:, block * rows : (block + 1) * rows] = ref[...]

    def multiply(step, carry):
        columns = pl.ds(pl.multiple_of(step * TILE, TILE), TILE)
        values = values_ref[...]
        by_real = jnp.dot(values, operator_ref[0, :, columns], preferred_element_type=jnp.float32)
        by_imag = jnp.dot(values, operator_ref[1, :, columns], preferred_element_type=jnp.float32)
        total = jnp.concatenate(
            [by_real[:width] - by_imag[width:], by_real[width:] + by_imag[:width]], axis=0
        ) + source_ref[:, columns].astype(jnp.float32)
        full_ref[:, columns] = total
        short_ref[:, columns] = total.astype(jnp.bfloat16)
        return carry

    lax.fori_loop(0, rows // TILE, multiply, 0)


def layer(blocks, operator, source):
    lanes, rows = source.shape
    vmem = pl.BlockSpec(memory_space=pltpu.VMEM)
    return pl.pallas_call(
        layer_kernel,
        out_shape=(
            jax.ShapeDtypeStruct((lanes, rows), jnp.float32),
            jax.ShapeDtypeStruct((lanes, rows), jnp.bfloat16),
        ),
        in_specs=[vmem] * (len(blocks) + 2),
        out_specs=(vmem, vmem),
        scratch_shapes=[pltpu.VMEM((lanes, len(blocks) * rows), jnp.bfloat16)],
        compiler_params=pltpu.CompilerParams(vmem_limit_bytes=VMEM_LIMIT),
        cost_estimate=pl.CostEstimate(
            flops=4 * len(blocks) * rows * rows * lanes, bytes_accessed=1 << 20, transcendentals=0
        ),
    )(*blocks, operator, source)


def batched(array, width):
    parts, rows, columns = array.shape
    split = array.reshape(parts, rows, columns // width, width)
    return jnp.transpose(split, (2, 0, 3, 1)).reshape(columns // width, parts * width, rows)


def unbatched(array, parts):
    count, lanes, rows = array.shape
    split = array.reshape(count, parts, lanes // parts, rows)
    return jnp.transpose(split, (1, 3, 0, 2)).reshape(parts, rows, count * lanes // parts)


def on_device(operator, sources, boundary):
    rows = operator.shape[2]
    total = sources.shape[3]
    layers = lax.axis_size("layer")
    devices = lax.axis_size("row")
    stages = layers // 2
    level = lax.axis_index("layer")
    core = level % 2
    stage = level // 2
    half = total // 2
    width = WIDTH
    count = half // width
    beats = count + stages - 1
    swap = [(i, i ^ 1) for i in range(layers)]

    def exchanged(value, distance):
        return lax.ppermute(value, "row", [(r, r ^ distance) for r in range(devices)])

    def onward(value, distance):
        if ONWARD:
            pairs = [
                (i * devices + r, (i + 2) % layers * devices + (r ^ distance))
                for i in range(layers)
                for r in range(devices)
            ]
            return lax.ppermute(value, ("layer", "row"), pairs)
        return lax.ppermute(value, "layer", [(i, (i + 2) % layers) for i in range(layers)])

    def spread(near, far):
        slots = {0: near}
        slots[1] = exchanged(near, 1)
        slots[3] = exchanged(near, 3)
        slots[2] = exchanged(near, 2)
        slots[4] = far
        slots[5] = exchanged(far, 1)
        slots[7] = exchanged(far, 3)
        slots[6] = exchanged(slots[2], 4)
        return [slots[slot] for slot in range(devices)]

    def turned_round(slots):
        return [slots[slot ^ 4] for slot in range(devices)]

    row = lax.axis_index("row").astype(jnp.int32)
    order = row ^ jnp.arange(devices, dtype=jnp.int32)
    own = transposed(order, operator[:, 0])
    other = lax.ppermute(own, "layer", swap)
    first_operator = jnp.where(core == 0, own, other)

    entering = batched(lax.dynamic_slice_in_dim(boundary, core * half, half, 2), width)
    opening_far = exchanged(entering[0], 4)
    entering_far = exchanged(entering[1:], 4)
    own_sources = sources[:, 0]
    mine = lax.dynamic_slice_in_dim(own_sources, core * half, half, 2)
    theirs = lax.ppermute(
        lax.dynamic_slice_in_dim(own_sources, (1 - core) * half, half, 2), "layer", swap
    )
    first_sources = batched(jnp.where(core == 0, mine, theirs), width)
    second_sources = batched(jnp.where(core == 0, theirs, mine), width)

    near = far = None
    firsts = jnp.zeros((count, 2 * width, rows), jnp.float32)
    seconds = jnp.zeros((count, 2 * width, rows), jnp.float32)
    for step in range(beats):
        batch = step - stage
        place = jnp.clip(batch, 0, count - 1)
        working = jnp.logical_and(batch >= 0, batch < count)
        if step == 0:
            slots = spread(entering[0], opening_far)
        else:
            if step < count:
                near = jnp.where(stage == 0, entering[step], near)
                far = jnp.where(stage == 0, entering_far[step - 1], far)
            slots = turned_round(spread(far, near))
        first, middle = layer(slots, first_operator, first_sources[place])
        if step == 0:
            later_own, later_other, _ = lax.optimization_barrier((own, other, middle))
            second_operator = jnp.where(core == 0, later_other, later_own)
        gathered = spread(middle, exchanged(middle, 4))
        second, leaving = layer(gathered, second_operator, second_sources[place])
        if step < beats - 1:
            near = onward(leaving, 0)
            far = onward(leaving, 4)
        first = jnp.where(working, first, firsts[place])
        second = jnp.where(working, second, seconds[place])
        firsts = lax.dynamic_update_index_in_dim(firsts, first, place, 0)
        seconds = lax.dynamic_update_index_in_dim(seconds, second, place, 0)

    kept = jnp.where(core == 0, firsts, seconds)
    given = lax.ppermute(jnp.where(core == 0, seconds, firsts), "layer", swap)
    kept = unbatched(kept, 2)
    given = unbatched(given, 2)
    low = jnp.where(core == 0, kept, given)
    high = jnp.where(core == 0, given, kept)
    return jnp.concatenate([low, high], axis=2)[:, None]


def solution(mesh):
    placed = (P(None, "layer", "row", None), P(None, "layer", "row", None), P(None, "row", None))
    return jax.shard_map(
        on_device,
        mesh=mesh,
        in_specs=placed,
        out_specs=P(None, "layer", "row", None),
        check_vma=False,
    )
```
